256 devices in a mesh: pair: 8 (over x, y_lo), row: 32 (over y_hi, z, core).
Axes of the slice: x: 4, y: 4 (y_hi: 2, y_lo: 2; y = y_hi * 2 + y_lo), z: 8, core: 2. Of those that a mesh axis runs over, the one named last changes fastest.
Arguments:
- matrix: float32 [2, 131072, 1024], P(None, 'row', 'pair'), may hold values from -100 to 100, as said below
Outputs:
- rotated_matrix: float32 [2, 131072, 1024], P(None, 'row', 'pair')
The draws below stay inside these ranges and needn't reach their ends.
Inputs may be any that keep to these rules, and one draw needn't show every extreme that they name: `matrix`: entries are real values with column blocks that are far from orthogonal to one another.
All inputs are finite; a program needn't handle non-finite values.
Results may differ from the reference program's by a relative error of at most 0.00014.
Values sent between devices are 32-bit elements; how exact they have to be, the bound alone decides.
A program may use at most 64 MiB of HBM per device.

```python
import math
import jax
import jax.numpy as jnp
from jax import lax

BW = 128
STEPS = 2
SWEEPS = 2
NEWTON = 3
COLS = 1024
ROWS = 131072
N_PAIR = 8


def draw_matrix(key, part):
    subkeys = jax.random.split(key, 5)
    row_scale = jnp.exp(jax.random.uniform(subkeys[0], (ROWS,), jnp.float32, math.log(0.3), math.log(3.0)))
    col_scale = jnp.exp(jax.random.uniform(subkeys[1], (2, 1, COLS), jnp.float32, math.log(0.3), math.log(3.0)))
    common = jnp.clip(jax.random.normal(subkeys[2], (ROWS,), jnp.float32), -3.0, 3.0)
    weight = jnp.clip(jax.random.normal(subkeys[3], (2, 1, COLS), jnp.float32), -3.0, 3.0)
    noise_part = jnp.clip(jax.random.normal(subkeys[4], (2, ROWS, COLS), jnp.float32), -4.0, 4.0)
    inner = 0.7 * common[None, :, None] * weight + noise_part
    return (row_scale[None, :, None] * col_scale * inner).astype(jnp.float32)


def setup_inputs(seed: int = 0) -> dict:
    seeds = jax.random.split(jax.random.key(seed), 2)
    matrix = draw_matrix(jax.random.fold_in(seeds[1], 71), 0)
    return dict(matrix=matrix)


def gram_of(left_cols, right_cols):
    return lax.dot_general(left_cols, right_cols, (((0,), (0,)), ((), ())), precision=lax.Precision.HIGHEST, preferred_element_type=jnp.float32)

def product(left_mat, right_mat):
    return jnp.dot(left_mat, right_mat, precision=lax.Precision.HIGHEST, preferred_element_type=jnp.float32)

def polar_turn(gram_matrix):
    half_width = gram_matrix.shape[0] // 2
    diagonal = jnp.diagonal(gram_matrix)
    inverse = 1.0 / jnp.sqrt(diagonal + 1e-06)
    cross_part = gram_matrix[:half_width, half_width:] * inverse[:half_width, None] * inverse[None, half_width:]
    cross_part = cross_part / (1.0 + jnp.sqrt(jnp.sum(cross_part * cross_part)))
    zero_block = jnp.zeros((half_width, half_width), jnp.float32)
    skew_part = jnp.concatenate([jnp.concatenate([zero_block, cross_part], 1), jnp.concatenate([-cross_part.T, zero_block], 1)], 0)
    identity = jnp.eye(2 * half_width, dtype=jnp.float32)
    factor = identity + skew_part
    for repeat in range(NEWTON):
        factor = product(factor, 1.5 * identity - 0.5 * gram_of(factor, factor))
    return factor

def pair_rotation(gram_matrix):
    rotation = jnp.eye(gram_matrix.shape[0], dtype=jnp.float32)
    current = gram_matrix
    for sweep_index in range(SWEEPS):
        factor = polar_turn(current)
        rotation = product(rotation, factor)
        if sweep_index + 1 < SWEEPS:
            current = gram_of(factor, product(current, factor))
    return rotation

def rotate_pair(blocks):
    upper_block, lower_block = blocks
    pair_cols = jnp.concatenate([upper_block, lower_block], 1)
    rotation = pair_rotation(gram_of(pair_cols, pair_cols))
    rotated = product(pair_cols, rotation)
    return (rotated[:, :BW], rotated[:, BW:])

def reference(matrix):
    row_total = matrix.shape[1]
    upper_stack = matrix[0].reshape(row_total, N_PAIR, BW).transpose(1, 0, 2)
    lower_stack = matrix[1].reshape(row_total, N_PAIR, BW).transpose(1, 0, 2)
    for step_index in range(STEPS):
        upper_stack, lower_stack = lax.map(rotate_pair, (upper_stack, lower_stack))
        new_upper = jnp.concatenate([upper_stack[0:1], lower_stack[0:1], upper_stack[1:N_PAIR - 1]], 0)
        new_lower = jnp.concatenate([lower_stack[1:], upper_stack[N_PAIR - 1:]], 0)
        upper_stack, lower_stack = (new_upper, new_lower)
    upper_flat = upper_stack.transpose(1, 0, 2).reshape(row_total, N_PAIR * BW)
    lower_flat = lower_stack.transpose(1, 0, 2).reshape(row_total, N_PAIR * BW)
    return jnp.stack([upper_flat, lower_flat], 0)
```

```python
import functools
import jax
import jax.numpy as jnp
from jax import lax
from jax.experimental import pallas as pl
from jax.experimental.pallas import tpu as pltpu
from jax.sharding import PartitionSpec as P

SWEEPS = 2
BW = 128
CHUNK = 512
MESH = pl.DeviceIdType.MESH
F32 = jnp.float32
BF16 = jnp.bfloat16

CHIPS = [(a, d) for d in (4, 3, 5, 2, 6, 1, 7, 0) for a in (1, 0) if (a, d) != (0, 0)]


def split(x):
    high = x.astype(BF16)
    return high, (x - high.astype(F32)).astype(BF16)


def mul(a, b, dims):
    return lax.dot_general(a, b, (dims, ((), ())), preferred_element_type=F32)


def mul3(a, b, dims=((1,), (0,))):
    ah, al = split(a)
    bh, bl = split(b)
    return mul(ah, bh, dims) + (mul(ah, bl, dims) + mul(al, bh, dims))


def mul6(a, b, dims=((1,), (0,))):
    return lax.dot_general(
        a, b, (dims, ((), ())), precision=lax.Precision.HIGHEST, preferred_element_type=F32
    )


small = mul6


def diag_mask():
    i = lax.broadcasted_iota(jnp.int32, (BW, BW), 0)
    j = lax.broadcasted_iota(jnp.int32, (BW, BW), 1)
    return i, j


def polar_even(t, eye):
    t2 = small(t, t)
    t3 = small(t2, t)
    t4 = small(t2, t2)
    e = 0.25 * t3 - 0.75 * t2
    m = eye - 0.5 * t + 0.375 * t2 - 0.3125 * t3 + 0.0625 * t4
    s = small(e, e)
    r = small(m, 0.375 * eye - 0.125 * e)
    return m + small(r, s)


def turn(cross, first_diag, second_diag, eye):
    c = cross * (1.0 / jnp.sqrt(first_diag + 1e-06)) * (1.0 / jnp.sqrt(second_diag + 1e-06))
    total = jnp.sum(jnp.sum(c * c, axis=1, keepdims=True), axis=0, keepdims=True)
    x = c / (1.0 + jnp.sqrt(total))
    xt = x.T
    a = polar_even(small(x, xt), eye)
    d = polar_even(small(xt, x), eye)
    b = small(a, x)
    return a, b, d


def whole(a, b, d):
    return jnp.concatenate(
        [jnp.concatenate([a, b], 1), jnp.concatenate([-b.T, d], 1)], 0
    )


def rotation(first, second, cross, first_diag, second_diag):
    i, j = diag_mask()
    eye = jnp.where(i == j, 1.0, 0.0).astype(F32)
    h = jnp.concatenate(
        [jnp.concatenate([first, cross], 1), jnp.concatenate([cross.T, second], 1)], 0
    )
    a, b, d = turn(cross, first_diag, second_diag, eye)
    y = whole(a, b, d)
    hy = small(h, y)
    new_cross = small(jnp.concatenate([a, -b], 1), hy[:, BW:])
    diag = jnp.sum(y * hy, axis=0, keepdims=True)
    new_first = jnp.sum(jnp.where(i == j, diag[:, :BW], 0.0), axis=1, keepdims=True)
    a, b, d = turn(new_cross, new_first, diag[:, BW:], eye)
    return h, small(y, whole(a, b, d))


def kernel(
    x_hbm, o_hbm,
    xin, xhi, xlo, own, far, out,
    pay, cbuf, dl, dlr, rsrc, rbuf, res, full, wbuf,
    gown, gfar, pay2, cbuf2, acc2, rbuf2, xsrc, xbuf, res2, full2,
    lsem, osem, cs, cr, rs_s, rs_r, ag_s, ag_r, fs, fr,
    ss, sr, gs, gr, cs2, cr2, rs2_s, rs2_r, xs, xr, ag2_s, ag2_r, fs2, fr2,
):
    p = lax.axis_index("pair")
    r = lax.axis_index("row")
    yh, z, c = r // 16, lax.rem(r // 2, 8), lax.rem(r, 2)
    chip = yh * 8 + z
    m = p // 2
    uc = lax.rem(m + 1, 2)
    half = lax.rem(m + p, 2)
    pu = jnp.where(p >= 2, p - 2, 1 - p)
    po = jnp.where(p <= 5, p + 2, 13 - p)
    partner = [jnp.where(uc == s, pu, po) for s in (0, 1)]
    mine = [jnp.where(uc == s, p == 0, p <= 6) for s in (0, 1)]
    lead = [jnp.where(uc == s, p != 1, p == 7) for s in (0, 1)]
    swap = jnp.logical_or(lax.rem(m, 2) == 1, p == 0)
    rows = x_hbm.shape[1]
    n_chunks = rows // CHUNK
    part = n_chunks // 2

    def chip_row(op, core):
        return lax.rem(yh + op[0], 2) * 16 + lax.rem(z + op[1], 8) * 2 + core

    def chip_index(op):
        return lax.rem(yh + op[0], 2) * 8 + lax.rem(z + op[1], 8)

    sibling = (p, chip_row((0, 0), 1 - c))
    peers = [(p, chip_row(op, c)) for op in CHIPS]

    def remote(src, dst, send, recv, device):
        return pltpu.make_async_remote_copy(
            src_ref=src, dst_ref=dst, send_sem=send, recv_sem=recv,
            device_id=device, device_id_type=MESH,
        )

    def load(k):
        return pltpu.make_async_copy(
            x_hbm.at[:, pl.ds(k * CHUNK, CHUNK)], xin.at[:, pl.ds(k * CHUNK, CHUNK)], lsem.at[k]
        )

    for k in range(n_chunks):
        load(k).start()
    barrier = pltpu.get_barrier_semaphore()
    everyone = [sibling] + peers + [(partner[0], r), (partner[1], r)]
    for device in everyone:
        pl.semaphore_signal(barrier, inc=1, device_id=device, device_id_type=MESH)

    def gram_chunk(k, g):
        load(k).wait()
        at = pl.ds(pl.multiple_of(k * CHUNK, CHUNK), CHUNK)
        high, low = split(jnp.concatenate([xin[0, at], xin[1, at]], 1))
        xhi[at] = high
        xlo[at] = low
        return g + mul(high, jnp.concatenate([high, low], 1), ((0,), (0,)))

    g = lax.fori_loop(0, n_chunks, gram_chunk, jnp.zeros((2 * BW, 4 * BW), F32))
    gl = g[:, 2 * BW:]
    g = g[:, :2 * BW] + (gl + gl.T)
    i, j = diag_mask()
    pay[0] = g[:BW, BW:]
    pay[1] = jnp.where(i >= j, g[:BW, :BW], g[BW:, BW:])
    low_diag = jnp.sum(jnp.where(i == j, g[BW:, BW:], 0.0), axis=0, keepdims=True)
    dl[...] = jnp.broadcast_to(low_diag, (8, BW))
    pl.semaphore_wait(barrier, len(everyone))

    c1 = remote(pay.at[1 - c], cbuf, cs.at[0], cr.at[0], sibling)
    c2 = remote(dl, dlr, cs.at[1], cr.at[1], sibling)
    c1.start()
    c2.start()
    c1.wait()
    c2.wait()
    rsrc[:, :8] = (pay[c] + cbuf[...]).reshape(16, 8, BW)
    rsrc[:, 8:] = jnp.broadcast_to((dl[...] + dlr[...])[None], (16, 8, BW))
    copies = []
    for n, op in enumerate(CHIPS):
        cp = remote(rsrc.at[chip_index(op)], rbuf.at[n], rs_s.at[n], rs_r.at[n], peers[n])
        cp.start()
        copies.append(cp)
    for cp in copies:
        cp.wait()
    total = rsrc[chip] + jnp.sum(rbuf[...], axis=0)
    low_diag = total[8:9]
    here = pl.ds(pl.multiple_of(chip * 8, 8), 8)
    res[here] = total[:8]
    copies = []
    for n, op in enumerate(CHIPS):
        cp = remote(res.at[here], res.at[here], ag_s.at[n], ag_r.at[n], peers[n])
        cp.start()
        copies.append(cp)
    for cp in copies:
        cp.wait()
    cp = remote(res, full.at[c], fs, fr, sibling)
    cp.start()
    full[c] = res[...]
    cp.wait()
    cross = full[0]
    packed = full[1]
    flipped = packed.T
    upper = jnp.where(i >= j, packed, flipped)
    lower = jnp.where(i == j, jnp.broadcast_to(low_diag, (BW, BW)), jnp.where(i < j, packed, flipped))
    up_diag = jnp.sum(jnp.where(i == j, upper, 0.0), axis=1, keepdims=True)
    h, v = rotation(upper, lower, cross, up_diag, low_diag)
    w = jnp.where(swap, jnp.concatenate([v[:, BW:], v[:, :BW]], 1), v)
    wh, wl = split(w)
    wbuf[0] = wh
    wbuf[1] = wl

    def send(k, s):
        at = pl.ds(pl.multiple_of(k * CHUNK, CHUNK), CHUNK)
        return remote(own.at[s, at], far.at[s, at], ss.at[s, k], sr.at[s, k], (partner[s], r))

    def product(k):
        at = pl.ds(pl.multiple_of(k * CHUNK, CHUNK), CHUNK)
        xh = xhi[at]
        dims = ((1,), (0,))
        y = mul(xh, wbuf[0], dims) + (mul(xh, wbuf[1], dims) + mul(xlo[at], wbuf[0], dims))
        own[0, at] = y[:, :BW]
        own[1, at] = y[:, BW:]

    def first_part(n, carry):
        k = half * part + n
        product(k)
        send(k, 0).start()
        send(k, 1).start()
        return carry

    lax.fori_loop(0, part, first_part, 0)

    hw = small(h, w)
    for s in (0, 1):
        gown[s] = small(w[:, s * BW:(s + 1) * BW].T, hw[:, s * BW:(s + 1) * BW])
    grams = [remote(gown.at[s], gfar.at[s], gs.at[s], gr.at[s], (partner[s], r)) for s in (0, 1)]
    for cp in grams:
        cp.start()

    def second_product(n, carry):
        product((1 - half) * part + n)
        return carry

    lax.fori_loop(0, part, second_product, 0)

    def cross_chunk(n, acc):
        k = (1 - half) * part + n
        at = pl.ds(pl.multiple_of(k * CHUNK, CHUNK), CHUNK)
        out_acc = []
        for s in (0, 1):
            send(k, s).wait_recv()
            lh, ll = split(own[s, at])
            fh, fl = split(far[s, at])
            dims = ((0,), (0,))
            q = mul(lh, jnp.concatenate([fh, fl], 1), dims)
            out_acc.append(acc[s] + (q[:, :BW] + (q[:, BW:] + mul(ll, fh, dims))))
        return tuple(out_acc)

    zero = jnp.zeros((BW, BW), F32)
    acc = lax.fori_loop(0, part, cross_chunk, (zero, zero))

    def second_send(n, carry):
        send(half * part + n, 0).wait_send()
        send(half * part + n, 1).wait_send()
        return carry

    lax.fori_loop(0, part, second_send, 0)
    for s in (0, 1):
        pay2[s] = jnp.where(mine[s], acc[s], acc[s].T)
    cp = remote(pay2.at[1 - c], cbuf2, cs2, cr2, sibling)
    cp.start()

    def second_start(n, carry):
        k = (1 - half) * part + n
        send(k, 0).start()
        send(k, 1).start()
        return carry

    lax.fori_loop(0, part, second_start, 0)
    cp.wait()
    acc2[...] = pay2[c] + cbuf2[...]
    copies = []
    for n, op in enumerate(CHIPS):
        at = pl.ds(pl.multiple_of(chip_index(op) * 8, 8), 8)
        cp = remote(acc2.at[at], rbuf2.at[n], rs2_s.at[n], rs2_r.at[n], peers[n])
        cp.start()
        copies.append(cp)
    for cp in copies:
        cp.wait()
    xsrc[...] = acc2[here] + jnp.sum(rbuf2[...], axis=0)
    edge = jnp.where(c == 0, partner[0], partner[1])
    cp = remote(xsrc, xbuf, xs, xr, (edge, r))
    cp.start()
    cp.wait()
    res2[here] = xsrc[...] + xbuf[...]
    copies = []
    for n, op in enumerate(CHIPS):
        cp = remote(res2.at[here], res2.at[here], ag2_s.at[n], ag2_r.at[n], peers[n])
        cp.start()
        copies.append(cp)
    for cp in copies:
        cp.wait()
    cp = remote(res2, full2.at[c], fs2, fr2, sibling)
    cp.start()
    full2[c] = res2[...]
    for q in grams:
        q.wait()
    cp.wait()

    weights = []
    for s in (0, 1):
        first = jnp.where(mine[s], gown[s], gfar[s])
        second = jnp.where(mine[s], gfar[s], gown[s])
        fd = jnp.sum(jnp.where(i == j, first, 0.0), axis=1, keepdims=True)
        sd = jnp.sum(jnp.where(i == j, second, 0.0), axis=0, keepdims=True)
        _, v = rotation(first, second, full2[s], fd, sd)
        v = jnp.where(lead[s], v[:, :BW], v[:, BW:])
        v = jnp.where(mine[s], v, jnp.concatenate([v[BW:], v[:BW]], 0))
        weights.append(split(v))

    def store(k, s):
        at = pl.ds(pl.multiple_of(k * CHUNK, CHUNK), CHUNK)
        slot = jnp.where(uc == s, 0, 1)
        return pltpu.make_async_copy(out.at[s, at], o_hbm.at[slot, at], osem.at[s, k])

    def last_product(k):
        at = pl.ds(pl.multiple_of(k * CHUNK, CHUNK), CHUNK)
        dims = ((1,), (0,))
        for s in (0, 1):
            vh, vl = weights[s]
            bh, bl = split(jnp.concatenate([own[s, at], far[s, at]], 1))
            out[s, at] = mul(bh, vh, dims) + (mul(bh, vl, dims) + mul(bl, vh, dims))
            store(k, s).start()

    def last_a(n, carry):
        last_product((1 - half) * part + n)
        return carry

    lax.fori_loop(0, part, last_a, 0)

    def last_b(n, carry):
        k = half * part + n
        send(k, 0).wait_recv()
        send(k, 1).wait_recv()
        last_product(k)
        return carry

    lax.fori_loop(0, part, last_b, 0)

    def finish(k, carry):
        store(k, 0).wait()
        store(k, 1).wait()
        return carry

    lax.fori_loop(0, n_chunks, finish, 0)

    def finish_send(n, carry):
        k = (1 - half) * part + n
        send(k, 0).wait_send()
        send(k, 1).wait_send()
        return carry

    lax.fori_loop(0, part, finish_send, 0)


def body(matrix):
    rows = matrix.shape[1]
    n_chunks = rows // CHUNK
    dma = pltpu.SemaphoreType.DMA
    n = len(CHIPS)
    block = pltpu.VMEM((2, rows, BW), F32)
    square = pltpu.VMEM((BW, BW), F32)
    squares = pltpu.VMEM((2, BW, BW), F32)
    tile = pltpu.VMEM((8, BW), F32)
    scratch = [
        block, pltpu.VMEM((rows, 2 * BW), BF16), pltpu.VMEM((rows, 2 * BW), BF16), block, block, block,
        squares, square, tile, tile, pltpu.VMEM((16, 16, BW), F32), pltpu.VMEM((n, 16, BW), F32),
        square, squares, pltpu.VMEM((2, 2 * BW, 2 * BW), BF16),
        squares, squares, squares, square, square, pltpu.VMEM((n, 8, BW), F32), tile, tile, square, squares,
        dma((n_chunks,)), dma((2, n_chunks)), dma((2,)), dma((2,)), dma((n,)), dma((n,)), dma((n,)), dma((n,)),
        dma, dma, dma((2, n_chunks)), dma((2, n_chunks)), dma((2,)), dma((2,)), dma, dma, dma((n,)), dma((n,)),
        dma, dma, dma((n,)), dma((n,)), dma, dma,
    ]
    return pl.pallas_call(
        kernel,
        out_shape=jax.ShapeDtypeStruct(matrix.shape, F32),
        in_specs=[pl.BlockSpec(memory_space=pl.ANY)],
        out_specs=pl.BlockSpec(memory_space=pl.ANY),
        scratch_shapes=scratch,
        compiler_params=pltpu.CompilerParams(
            collective_id=0, has_side_effects=True, vmem_limit_bytes=48 << 20
        ),
    )(matrix)


def solution(mesh):
    specs = P(None, "row", "pair")
    return jax.shard_map(body, mesh=mesh, in_specs=(specs,), out_specs=specs, check_vma=False)
```

```python
import functools
import jax
import jax.numpy as jnp
from jax import lax
from jax.experimental import pallas as pl
from jax.experimental.pallas import tpu as pltpu
from jax.sharding import PartitionSpec as P

SWEEPS = 2
BW = 128
CHUNK = 256
EARLY = 3
PACE = (1, 2, 2, 3)
LAST = 2
MESH = pl.DeviceIdType.MESH
F32 = jnp.float32
BF16 = jnp.bfloat16

CHIPS = [(a, d) for d in (4, 3, 5, 2, 6, 1, 7, 0) for a in (1, 0) if (a, d) != (0, 0)]


def split(x):
    high = x.astype(BF16)
    return high, (x - high.astype(F32)).astype(BF16)


def mul(a, b, dims):
    return lax.dot_general(a, b, (dims, ((), ())), preferred_element_type=F32)


def mul3(a, b, dims=((1,), (0,))):
    ah, al = split(a)
    bh, bl = split(b)
    return mul(ah, bh, dims) + (mul(ah, bl, dims) + mul(al, bh, dims))


def mul6(a, b, dims=((1,), (0,))):
    return lax.dot_general(
        a, b, (dims, ((), ())), precision=lax.Precision.HIGHEST, preferred_element_type=F32
    )


small = mul6


def diag_mask():
    i = lax.broadcasted_iota(jnp.int32, (BW, BW), 0)
    j = lax.broadcasted_iota(jnp.int32, (BW, BW), 1)
    return i, j


def polar_even(ts, eye):
    t2 = [small(t, t) for t in ts]
    t3 = [small(u, t) for u, t in zip(t2, ts)]
    t4 = [small(u, u) for u in t2]
    e = [0.25 * w - 0.75 * u for w, u in zip(t3, t2)]
    m = [
        eye - 0.5 * t + 0.375 * u - 0.3125 * w + 0.0625 * q
        for t, u, w, q in zip(ts, t2, t3, t4)
    ]
    s = [small(u, u) for u in e]
    r = [small(w, 0.375 * eye - 0.125 * u) for w, u in zip(m, e)]
    return [w + small(u, q) for w, u, q in zip(m, r, s)]


def turn(items, eye):
    cs = [
        cross * (1.0 / jnp.sqrt(fd + 1e-06)) * (1.0 / jnp.sqrt(sd + 1e-06))
        for cross, fd, sd in items
    ]
    totals = [jnp.sum(jnp.sum(c * c, axis=1, keepdims=True), axis=0, keepdims=True) for c in cs]
    xs = [c / (1.0 + jnp.sqrt(total)) for c, total in zip(cs, totals)]
    xts = [x.T for x in xs]
    ts = [small(x, xt) for x, xt in zip(xs, xts)] + [small(xt, x) for x, xt in zip(xs, xts)]
    evens = polar_even(ts, eye)
    n = len(items)
    return [(evens[k], small(evens[k], xs[k]), evens[n + k]) for k in range(n)]


def whole(a, b, d):
    return jnp.concatenate([jnp.concatenate([a, b], 1), jnp.concatenate([-b.T, d], 1)], 0)


def rotations(items):
    i, j = diag_mask()
    eye = jnp.where(i == j, 1.0, 0.0).astype(F32)
    hs = [
        jnp.concatenate([jnp.concatenate([f, c], 1), jnp.concatenate([c.T, s], 1)], 0)
        for f, s, c, _, _ in items
    ]
    turns = turn([item[2:] for item in items], eye)
    ys = [whole(*t) for t in turns]
    hys = [small(h, y) for h, y in zip(hs, ys)]
    crosses = [
        small(jnp.concatenate([a, -b], 1), hy[:, BW:]) for (a, b, _), hy in zip(turns, hys)
    ]
    diags = [jnp.sum(y * hy, axis=0, keepdims=True) for y, hy in zip(ys, hys)]
    firsts = [
        jnp.sum(jnp.where(i == j, diag[:, :BW], 0.0), axis=1, keepdims=True) for diag in diags
    ]
    turns = turn(
        [(c, f, diag[:, BW:]) for c, f, diag in zip(crosses, firsts, diags)], eye
    )
    return [(h, small(y, whole(*t))) for h, y, t in zip(hs, ys, turns)]


def kernel(
    x_hbm, o_hbm,
    xin, xhi, xlo, own, far, out, bhi, blo,
    pay, cbuf, dl, dlr, rsrc, rbuf, res, full, wbuf,
    ebuf, wown, wfar, gown, gfar, pay2, cbuf2, acc2, rbuf2, res2, full2,
    lsem, osem, cs, cr, rs_s, rs_r, ag_s, ag_r, fs, fr,
    es, er, ws, wr, ss, sr, gs, gr, cs2, cr2, rs2_s, rs2_r, ag2_s, ag2_r, fs2, fr2,
):
    p = lax.axis_index("pair")
    r = lax.axis_index("row")
    yh, z, c = r // 16, lax.rem(r // 2, 8), lax.rem(r, 2)
    chip = yh * 8 + z
    m = p // 2
    uc = lax.rem(m + 1, 2)
    half = lax.rem(m + p, 2)
    pu = jnp.where(p >= 2, p - 2, 1 - p)
    po = jnp.where(p <= 5, p + 2, 13 - p)
    partner = [jnp.where(uc == s, pu, po) for s in (0, 1)]
    mine = [jnp.where(uc == s, p == 0, p <= 6) for s in (0, 1)]
    lead = [jnp.where(uc == s, p != 1, p == 7) for s in (0, 1)]
    swap = jnp.logical_or(lax.rem(m, 2) == 1, p == 0)
    rows = x_hbm.shape[1]
    n_chunks = rows // CHUNK
    part = n_chunks // 2

    def chip_row(op, core):
        return lax.rem(yh + op[0], 2) * 16 + lax.rem(z + op[1], 8) * 2 + core

    def chip_index(op):
        return lax.rem(yh + op[0], 2) * 8 + lax.rem(z + op[1], 8)

    sibling = (p, chip_row((0, 0), 1 - c))
    peers = [(p, chip_row(op, c)) for op in CHIPS]

    def remote(src, dst, send, recv, device):
        return pltpu.make_async_remote_copy(
            src_ref=src, dst_ref=dst, send_sem=send, recv_sem=recv,
            device_id=device, device_id_type=MESH,
        )

    def load(k):
        return pltpu.make_async_copy(
            x_hbm.at[:, pl.ds(k * CHUNK, CHUNK)], xin.at[:, pl.ds(k * CHUNK, CHUNK)], lsem.at[k]
        )

    def early(n, s):
        src = pl.ds(pl.multiple_of((half * part + n) * CHUNK, CHUNK), CHUNK)
        dst = pl.ds(n * CHUNK, CHUNK)
        return remote(xin.at[:, src], ebuf.at[s, :, dst], es.at[s, n], er.at[s, n], (partner[s], r))

    for k in range(n_chunks):
        load(k).start()
    barrier = pltpu.get_barrier_semaphore()
    aside = sibling[1]
    near = jnp.where(c == 0, partner[0], partner[1])
    other = jnp.where(c == 0, partner[1], partner[0])
    everyone = [sibling] + peers + [(partner[0], r), (partner[1], r), (near, aside)]
    for device in everyone:
        pl.semaphore_signal(barrier, inc=1, device_id=device, device_id_type=MESH)

    def gram_chunk(k, g):
        load(k).wait()
        at = pl.ds(pl.multiple_of(k * CHUNK, CHUNK), CHUNK)
        high, low = split(jnp.concatenate([xin[0, at], xin[1, at]], 1))
        xhi[at] = high
        xlo[at] = low
        return g + mul(high, jnp.concatenate([high, low], 1), ((0,), (0,)))

    g = lax.fori_loop(0, n_chunks, gram_chunk, jnp.zeros((2 * BW, 4 * BW), F32))
    gl = g[:, 2 * BW:]
    g = g[:, :2 * BW] + (gl + gl.T)
    i, j = diag_mask()
    pay[0] = g[:BW, BW:]
    pay[1] = jnp.where(i >= j, g[:BW, :BW], g[BW:, BW:])
    low_diag = jnp.sum(jnp.where(i == j, g[BW:, BW:], 0.0), axis=0, keepdims=True)
    dl[...] = jnp.broadcast_to(low_diag, (8, BW))
    pl.semaphore_wait(barrier, len(everyone))

    c1 = remote(pay.at[1 - c], cbuf, cs.at[0], cr.at[0], sibling)
    c2 = remote(dl, dlr, cs.at[1], cr.at[1], sibling)
    c1.start()
    c2.start()
    c1.wait()
    c2.wait()
    rsrc[:, :8] = (pay[c] + cbuf[...]).reshape(16, 8, BW)
    rsrc[:, 8:] = jnp.broadcast_to((dl[...] + dlr[...])[None], (16, 8, BW))
    copies = []
    for n, op in enumerate(CHIPS):
        cp = remote(rsrc.at[chip_index(op)], rbuf.at[n], rs_s.at[n], rs_r.at[n], peers[n])
        cp.start()
        copies.append(cp)
    early(0, 0).start()
    early(0, 1).start()
    for cp in copies:
        cp.wait()
    total = rsrc[chip] + jnp.sum(rbuf[...], axis=0)
    low_diag = total[8:9]
    here = pl.ds(pl.multiple_of(chip * 8, 8), 8)
    res[here] = total[:8]
    copies = []
    for n, op in enumerate(CHIPS):
        cp = remote(res.at[here], res.at[here], ag_s.at[n], ag_r.at[n], peers[n])
        cp.start()
        copies.append(cp)
    early(1, 0).start()
    early(1, 1).start()
    for cp in copies:
        cp.wait()
    cp = remote(res, full.at[c], fs, fr, sibling)
    cp.start()
    for n in range(2, EARLY):
        early(n, 0).start()
        early(n, 1).start()
    full[c] = res[...]
    cp.wait()
    cross = full[0]
    packed = full[1]
    flipped = packed.T
    upper = jnp.where(i >= j, packed, flipped)
    lower = jnp.where(i == j, jnp.broadcast_to(low_diag, (BW, BW)), jnp.where(i < j, packed, flipped))
    up_diag = jnp.sum(jnp.where(i == j, upper, 0.0), axis=1, keepdims=True)
    [(h, v)] = rotations([(upper, lower, cross, up_diag, low_diag)])
    w = jnp.where(swap, jnp.concatenate([v[:, BW:], v[:, :BW]], 1), v)
    wh, wl = split(w)
    wbuf[0] = wh
    wbuf[1] = wl

    for s in (0, 1):
        wown[s] = w[:, s * BW:(s + 1) * BW]
    turns = [remote(wown.at[s], wfar.at[s], ws.at[s], wr.at[s], (partner[s], r)) for s in (0, 1)]
    for cp in turns:
        cp.start()

    def send(k, s):
        at = pl.ds(pl.multiple_of(k * CHUNK, CHUNK), CHUNK)
        return remote(own.at[s, at], far.at[s, at], ss.at[s, k], sr.at[s, k], (partner[s], r))

    def product(at):
        xh = xhi[at]
        dims = ((1,), (0,))
        y = mul(xh, wbuf[0], dims) + (mul(xh, wbuf[1], dims) + mul(xlo[at], wbuf[0], dims))
        yh, yl = split(y)
        for s in (0, 1):
            cols = slice(s * BW, (s + 1) * BW)
            own[s, at] = y[:, cols]
            bhi[s, at, :BW] = yh[:, cols]
            blo[s, at, :BW] = yl[:, cols]

    def rows_at(begin, count):
        return pl.ds(pl.multiple_of(begin * CHUNK, CHUNK), count * CHUNK)

    def first_part(n, carry):
        k = half * part + n
        product(rows_at(k, 1))
        send(k, 0).start()
        send(k, 1).start()
        return carry

    lax.fori_loop(EARLY, part, first_part, 0)

    hw = small(h, w)
    for s in (0, 1):
        gown[s] = small(w[:, s * BW:(s + 1) * BW].T, hw[:, s * BW:(s + 1) * BW])

    grams = [remote(gown.at[s], gfar.at[s], gs.at[s], gr.at[s], (partner[s], r)) for s in (0, 1)]
    for cp in grams:
        cp.start()

    def second_product(n, carry):
        product(rows_at((1 - half) * part + n * (part // 2), part // 2))
        return carry

    lax.fori_loop(0, 2, second_product, 0)
    product(rows_at(half * part, EARLY))

    def cross(k, acc):
        at = pl.ds(pl.multiple_of(k * CHUNK, CHUNK), CHUNK)
        out_acc = []
        for s in (0, 1):
            lh, ll = bhi[s, at, :BW], blo[s, at, :BW]
            fh, fl = split(far[s, at])
            bhi[s, at, BW:] = fh
            blo[s, at, BW:] = fl
            dims = ((0,), (0,))
            q = mul(lh, jnp.concatenate([fh, fl], 1), dims)
            out_acc.append(acc[s] + (q[:, :BW] + (q[:, BW:] + mul(ll, fh, dims))))
        return tuple(out_acc)

    for cp in turns:
        cp.wait_recv()
    wparts = []
    for s in (0, 1):
        fh, fl = split(wfar[s])
        wparts.append((fh, jnp.concatenate([fh, fl], 1)))

    def early_chunk(n, acc):
        k = (1 - half) * part + n
        at = pl.ds(pl.multiple_of(k * CHUNK, CHUNK), CHUNK)
        came = pl.ds(pl.multiple_of(n * CHUNK, CHUNK), CHUNK)
        dims = ((1,), (0,))
        for s in (0, 1):
            early(n, s).wait_recv()
            eh, el = split(jnp.concatenate([ebuf[s, 0, came], ebuf[s, 1, came]], 1))
            q = mul(eh, wparts[s][1], dims)
            far[s, at] = q[:, :BW] + (q[:, BW:] + mul(el, wparts[s][0], dims))
        return cross(k, acc)

    def cross_chunk(n, acc):
        k = (1 - half) * part + n
        send(k, 0).wait_recv()
        send(k, 1).wait_recv()
        return cross(k, acc)

    zero = jnp.zeros((BW, BW), F32)
    acc = lax.fori_loop(0, EARLY, early_chunk, (zero, zero))
    acc = lax.fori_loop(EARLY, part, cross_chunk, acc)

    def first_wait(n, carry):
        send(half * part + n, 0).wait_send()
        send(half * part + n, 1).wait_send()
        return carry

    def early_wait(n, carry):
        early(n, 0).wait_send()
        early(n, 1).wait_send()
        return carry

    lax.fori_loop(EARLY, part, first_wait, 0)
    lax.fori_loop(0, EARLY, early_wait, 0)
    for cp in turns:
        cp.wait_send()
    for s in (0, 1):
        pay2[s] = jnp.where(mine[s], acc[s], acc[s].T)
    copies = [
        remote(pay2.at[c], cbuf2.at[0], cs2.at[0], cr2.at[0], (near, r)),
        remote(pay2.at[1 - c], cbuf2.at[1], cs2.at[1], cr2.at[1], (other, aside)),
        remote(pay2.at[1 - c], cbuf2.at[2], cs2.at[2], cr2.at[2], sibling),
    ]
    for cp in copies:
        cp.start()

    def second_start(step):
        begin = sum(PACE[:step])
        for n in range(begin, begin + PACE[step]):
            k = (1 - half) * part + n
            send(k, 0).start()
            send(k, 1).start()

    second_start(0)
    for cp in copies:
        cp.wait()
    acc2[...] = (pay2[c] + cbuf2[2]) + (cbuf2[0] + cbuf2[1])
    copies = []
    for n, op in enumerate(CHIPS):
        at = pl.ds(pl.multiple_of(chip_index(op) * 8, 8), 8)
        cp = remote(acc2.at[at], rbuf2.at[n], rs2_s.at[n], rs2_r.at[n], peers[n])
        cp.start()
        copies.append(cp)
    second_start(1)
    for cp in copies:
        cp.wait()
    res2[here] = acc2[here] + jnp.sum(rbuf2[...], axis=0)
    copies = []
    for n, op in enumerate(CHIPS):
        cp = remote(res2.at[here], res2.at[here], ag2_s.at[n], ag2_r.at[n], peers[n])
        cp.start()
        copies.append(cp)
    second_start(2)
    for cp in copies:
        cp.wait()
    cp = remote(res2, full2.at[c], fs2, fr2, sibling)
    cp.start()
    second_start(3)
    full2[c] = res2[...]
    for q in grams:
        q.wait()
    cp.wait()

    items = []
    for s in (0, 1):
        first = jnp.where(mine[s], gown[s], gfar[s])
        second = jnp.where(mine[s], gfar[s], gown[s])
        fd = jnp.sum(jnp.where(i == j, first, 0.0), axis=1, keepdims=True)
        sd = jnp.sum(jnp.where(i == j, second, 0.0), axis=0, keepdims=True)
        items.append((first, second, full2[s], fd, sd))
    weights = []
    for s, (_, v) in enumerate(rotations(items)):
        v = jnp.where(lead[s], v[:, :BW], v[:, BW:])
        v = jnp.where(mine[s], v, jnp.concatenate([v[BW:], v[:BW]], 0))
        vh, vl = split(v)
        weights.append((vh, jnp.concatenate([vh, vl], 1)))

    def store(begin, count, s):
        at = rows_at(begin, count)
        slot = jnp.where(uc == s, 0, 1)
        return pltpu.make_async_copy(out.at[s, at], o_hbm.at[slot, at], osem.at[s, begin])

    def last_product(begin, count):
        at = rows_at(begin, count)
        dims = ((1,), (0,))
        for s in (0, 1):
            vh, vhl = weights[s]
            q = mul(bhi[s, at], vhl, dims)
            out[s, at] = q[:, :BW] + (q[:, BW:] + mul(blo[s, at], vh, dims))
            store(begin, count, s).start()

    def last_a(n, carry):
        last_product((1 - half) * part + n * (part // 2), part // 2)
        return carry

    lax.fori_loop(0, 2, last_a, 0)

    def last_b(n, carry):
        begin = half * part + n * LAST
        at = rows_at(begin, LAST)
        for k in range(LAST):
            send(begin + k, 0).wait_recv()
            send(begin + k, 1).wait_recv()
        for s in (0, 1):
            fh, fl = split(far[s, at])
            bhi[s, at, BW:] = fh
            blo[s, at, BW:] = fl
        last_product(begin, LAST)
        return carry

    lax.fori_loop(0, part // LAST, last_b, 0)

    def finish_a(n, carry):
        for s in (0, 1):
            store((1 - half) * part + n * (part // 2), part // 2, s).wait()
        return carry

    def finish_b(n, carry):
        for s in (0, 1):
            store(half * part + n * LAST, LAST, s).wait()
        return carry

    lax.fori_loop(0, 2, finish_a, 0)
    lax.fori_loop(0, part // LAST, finish_b, 0)

    def finish_send(n, carry):
        k = (1 - half) * part + n
        send(k, 0).wait_send()
        send(k, 1).wait_send()
        return carry

    lax.fori_loop(0, part, finish_send, 0)


def body(matrix):
    rows = matrix.shape[1]
    n_chunks = rows // CHUNK
    dma = pltpu.SemaphoreType.DMA
    n = len(CHIPS)
    block = pltpu.VMEM((2, rows, BW), F32)
    square = pltpu.VMEM((BW, BW), F32)
    squares = pltpu.VMEM((2, BW, BW), F32)
    tile = pltpu.VMEM((8, BW), F32)
    scratch = [
        block, pltpu.VMEM((rows, 2 * BW), BF16), pltpu.VMEM((rows, 2 * BW), BF16), block, block, block,
        pltpu.VMEM((2, rows, 2 * BW), BF16), pltpu.VMEM((2, rows, 2 * BW), BF16),
        squares, square, tile, tile, pltpu.VMEM((16, 16, BW), F32), pltpu.VMEM((n, 16, BW), F32),
        square, squares, pltpu.VMEM((2, 2 * BW, 2 * BW), BF16),
        pltpu.VMEM((2, 2, EARLY * CHUNK, BW), F32), pltpu.VMEM((2, 2 * BW, BW), F32), pltpu.VMEM((2, 2 * BW, BW), F32),
        squares, squares, squares, pltpu.VMEM((3, BW, BW), F32), square, pltpu.VMEM((n, 8, BW), F32), square, squares,
        dma((n_chunks,)), dma((2, n_chunks)), dma((2,)), dma((2,)), dma((n,)), dma((n,)), dma((n,)), dma((n,)),
        dma, dma, dma((2, EARLY)), dma((2, EARLY)), dma((2,)), dma((2,)),
        dma((2, n_chunks)), dma((2, n_chunks)), dma((2,)), dma((2,)), dma((3,)), dma((3,)),
        dma((n,)), dma((n,)), dma((n,)), dma((n,)), dma, dma,
    ]
    return pl.pallas_call(
        kernel,
        out_shape=jax.ShapeDtypeStruct(matrix.shape, F32),
        in_specs=[pl.BlockSpec(memory_space=pl.ANY)],
        out_specs=pl.BlockSpec(memory_space=pl.ANY),
        scratch_shapes=scratch,
        compiler_params=pltpu.CompilerParams(
            collective_id=0, has_side_effects=True, vmem_limit_bytes=48 << 20
        ),
    )(matrix)


def solution(mesh):
    specs = P(None, "row", "pair")
    return jax.shard_map(body, mesh=mesh, in_specs=(specs,), out_specs=specs, check_vma=False)
```

```python
import functools
import jax
import jax.numpy as jnp
from jax import lax
from jax.experimental import pallas as pl
from jax.experimental.pallas import tpu as pltpu
from jax.sharding import PartitionSpec as P

SWEEPS = 2
BW = 128
CHUNK = 256
EARLY = 3
PACE = (1, 1, 2, 3, 1)
LEAD = 2
LAST = 2
MESH = pl.DeviceIdType.MESH
F32 = jnp.float32
BF16 = jnp.bfloat16

CHIPS = [(a, d) for d in (4, 3, 5, 2, 6, 1, 7, 0) for a in (1, 0) if (a, d) != (0, 0)]


def split(x):
    high = x.astype(BF16)
    return high, (x - high.astype(F32)).astype(BF16)


def mul(a, b, dims):
    return lax.dot_general(a, b, (dims, ((), ())), preferred_element_type=F32)


def mul3(a, b, dims=((1,), (0,))):
    ah, al = split(a)
    bh, bl = split(b)
    return mul(ah, bh, dims) + (mul(ah, bl, dims) + mul(al, bh, dims))


def mul6(a, b, dims=((1,), (0,))):
    return lax.dot_general(
        a, b, (dims, ((), ())), precision=lax.Precision.HIGHEST, preferred_element_type=F32
    )


small = mul3


def diag_mask():
    i = lax.broadcasted_iota(jnp.int32, (BW, BW), 0)
    j = lax.broadcasted_iota(jnp.int32, (BW, BW), 1)
    return i, j


def polar_even(ts, eye):
    t2 = [small(t, t) for t in ts]
    t3 = [small(u, t) for u, t in zip(t2, ts)]
    t4 = [small(u, u) for u in t2]
    e = [0.25 * w - 0.75 * u for w, u in zip(t3, t2)]
    m = [
        eye - 0.5 * t + 0.375 * u - 0.3125 * w + 0.0625 * q
        for t, u, w, q in zip(ts, t2, t3, t4)
    ]
    s = [small(u, u) for u in e]
    r = [small(w, 0.375 * eye - 0.125 * u) for w, u in zip(m, e)]
    return [w + small(u, q) for w, u, q in zip(m, r, s)]


def turn(items, eye):
    cs = [
        cross * (1.0 / jnp.sqrt(fd + 1e-06)) * (1.0 / jnp.sqrt(sd + 1e-06))
        for cross, fd, sd in items
    ]
    totals = [jnp.sum(jnp.sum(c * c, axis=1, keepdims=True), axis=0, keepdims=True) for c in cs]
    xs = [c / (1.0 + jnp.sqrt(total)) for c, total in zip(cs, totals)]
    xts = [x.T for x in xs]
    ts = [small(x, xt) for x, xt in zip(xs, xts)] + [small(xt, x) for x, xt in zip(xs, xts)]
    evens = polar_even(ts, eye)
    n = len(items)
    return [(evens[k], small(evens[k], xs[k]), evens[n + k]) for k in range(n)]


def whole(a, b, d):
    return jnp.concatenate([jnp.concatenate([a, b], 1), jnp.concatenate([-b.T, d], 1)], 0)


def rotations(items):
    i, j = diag_mask()
    eye = jnp.where(i == j, 1.0, 0.0).astype(F32)
    hs = [
        jnp.concatenate([jnp.concatenate([f, c], 1), jnp.concatenate([c.T, s], 1)], 0)
        for f, s, c, _, _ in items
    ]
    turns = turn([item[2:] for item in items], eye)
    ys = [whole(*t) for t in turns]
    hys = [small(h, y) for h, y in zip(hs, ys)]
    crosses = [
        small(jnp.concatenate([a, -b], 1), hy[:, BW:]) for (a, b, _), hy in zip(turns, hys)
    ]
    diags = [jnp.sum(y * hy, axis=0, keepdims=True) for y, hy in zip(ys, hys)]
    firsts = [
        jnp.sum(jnp.where(i == j, diag[:, :BW], 0.0), axis=1, keepdims=True) for diag in diags
    ]
    turns = turn(
        [(c, f, diag[:, BW:]) for c, f, diag in zip(crosses, firsts, diags)], eye
    )
    return [(h, small(y, whole(*t))) for h, y, t in zip(hs, ys, turns)]


def kernel(
    x_hbm, o_ref,
    xin, xhi, xlo, own, far, bhi, blo,
    pay, cbuf, dl, dlr, rsrc, rbuf, res, full, wbuf,
    ebuf, wown, wfar, gown, gfar, pay2, cbuf2, acc2, rbuf2, res2, full2,
    lsem, cs, cr, rs_s, rs_r, ag_s, ag_r, fs, fr,
    es, er, ws, wr, ws2, wr2, ss, sr, gs, gr, gs2, gr2, cs2, cr2, rs2_s, rs2_r, ag2_s, ag2_r, fs2, fr2,
):
    p = lax.axis_index("pair")
    r = lax.axis_index("row")
    yh, z, c = r // 16, lax.rem(r // 2, 8), lax.rem(r, 2)
    chip = yh * 8 + z
    m = p // 2
    uc = lax.rem(m + 1, 2)
    half = lax.rem(m + p, 2)
    pu = jnp.where(p >= 2, p - 2, 1 - p)
    po = jnp.where(p <= 5, p + 2, 13 - p)
    partner = [jnp.where(uc == s, pu, po) for s in (0, 1)]
    mine = [jnp.where(uc == s, p == 0, p <= 6) for s in (0, 1)]
    lead = [jnp.where(uc == s, p != 1, p == 7) for s in (0, 1)]
    swap = jnp.logical_or(lax.rem(m, 2) == 1, p == 0)
    rows = x_hbm.shape[1]
    n_chunks = rows // CHUNK
    part = n_chunks // 2

    def chip_row(op, core):
        return lax.rem(yh + op[0], 2) * 16 + lax.rem(z + op[1], 8) * 2 + core

    def chip_index(op):
        return lax.rem(yh + op[0], 2) * 8 + lax.rem(z + op[1], 8)

    sibling = (p, chip_row((0, 0), 1 - c))
    peers = [(p, chip_row(op, c)) for op in CHIPS]

    def remote(src, dst, send, recv, device):
        return pltpu.make_async_remote_copy(
            src_ref=src, dst_ref=dst, send_sem=send, recv_sem=recv,
            device_id=device, device_id_type=MESH,
        )

    def load(k):
        return pltpu.make_async_copy(
            x_hbm.at[:, pl.ds(k * CHUNK, CHUNK)], xin.at[:, pl.ds(k * CHUNK, CHUNK)], lsem.at[k]
        )

    def early(n, s):
        src = pl.ds(pl.multiple_of((half * part + n) * CHUNK, CHUNK), CHUNK)
        dst = pl.ds(n * CHUNK, CHUNK)
        return remote(xin.at[:, src], ebuf.at[s, :, dst], es.at[s, n], er.at[s, n], (partner[s], r))

    for k in range(n_chunks):
        load(k).start()
    barrier = pltpu.get_barrier_semaphore()
    aside = sibling[1]
    near = jnp.where(c == 0, partner[0], partner[1])
    other = jnp.where(c == 0, partner[1], partner[0])
    everyone = [sibling] + peers + [(partner[0], r), (partner[1], r), (near, aside)]
    for device in everyone:
        pl.semaphore_signal(barrier, inc=1, device_id=device, device_id_type=MESH)

    def gram_chunk(k, g):
        load(k).wait()
        at = pl.ds(pl.multiple_of(k * CHUNK, CHUNK), CHUNK)
        high, low = split(jnp.concatenate([xin[0, at], xin[1, at]], 1))
        xhi[at] = high
        xlo[at] = low
        return g + mul(high, jnp.concatenate([high, low], 1), ((0,), (0,)))

    g = lax.fori_loop(0, n_chunks, gram_chunk, jnp.zeros((2 * BW, 4 * BW), F32))
    gl = g[:, 2 * BW:]
    g = g[:, :2 * BW] + (gl + gl.T)
    i, j = diag_mask()
    pay[0] = g[:BW, BW:]
    pay[1] = jnp.where(i >= j, g[:BW, :BW], g[BW:, BW:])
    low_diag = jnp.sum(jnp.where(i == j, g[BW:, BW:], 0.0), axis=0, keepdims=True)
    dl[...] = jnp.broadcast_to(low_diag, (8, BW))
    pl.semaphore_wait(barrier, len(everyone))

    c1 = remote(pay.at[1 - c], cbuf, cs.at[0], cr.at[0], sibling)
    c2 = remote(dl, dlr, cs.at[1], cr.at[1], sibling)
    c1.start()
    c2.start()
    c1.wait()
    c2.wait()
    rsrc[:, :8] = (pay[c] + cbuf[...]).reshape(16, 8, BW)
    rsrc[:, 8:] = jnp.broadcast_to((dl[...] + dlr[...])[None], (16, 8, BW))
    copies = []
    for n, op in enumerate(CHIPS):
        cp = remote(rsrc.at[chip_index(op)], rbuf.at[n], rs_s.at[n], rs_r.at[n], peers[n])
        cp.start()
        copies.append(cp)
    early(0, 0).start()
    early(0, 1).start()
    for cp in copies:
        cp.wait()
    total = rsrc[chip] + jnp.sum(rbuf[...], axis=0)
    low_diag = total[8:9]
    here = pl.ds(pl.multiple_of(chip * 8, 8), 8)
    res[here] = total[:8]
    copies = []
    for n, op in enumerate(CHIPS):
        cp = remote(res.at[here], res.at[here], ag_s.at[n], ag_r.at[n], peers[n])
        cp.start()
        copies.append(cp)
    early(1, 0).start()
    early(1, 1).start()
    for cp in copies:
        cp.wait()
    cp = remote(res, full.at[c], fs, fr, sibling)
    cp.start()
    for n in range(2, EARLY):
        early(n, 0).start()
        early(n, 1).start()
    full[c] = res[...]
    cp.wait()
    cross = full[0]
    packed = full[1]
    flipped = packed.T
    upper = jnp.where(i >= j, packed, flipped)
    lower = jnp.where(i == j, jnp.broadcast_to(low_diag, (BW, BW)), jnp.where(i < j, packed, flipped))
    up_diag = jnp.sum(jnp.where(i == j, upper, 0.0), axis=1, keepdims=True)
    [(h, v)] = rotations([(upper, lower, cross, up_diag, low_diag)])
    w = jnp.where(swap, jnp.concatenate([v[:, BW:], v[:, :BW]], 1), v)
    wh, wl = split(w)
    wbuf[0] = wh
    wbuf[1] = wl

    for s in (0, 1):
        wown[s] = w[:, s * BW:(s + 1) * BW]
    wpart = pl.ds(pl.multiple_of(c * BW, BW), BW)
    turns = [
        remote(wown.at[s, wpart], wfar.at[s, wpart], ws.at[s], wr.at[s], (partner[s], r))
        for s in (0, 1)
    ]
    passed = [
        remote(wfar.at[s, wpart], wfar.at[s, wpart], ws2.at[s], wr2.at[s], sibling) for s in (0, 1)
    ]
    for cp in turns:
        cp.start()

    def send(k, s):
        at = pl.ds(pl.multiple_of(k * CHUNK, CHUNK), CHUNK)
        return remote(own.at[s, at], far.at[s, at], ss.at[s, k], sr.at[s, k], (partner[s], r))

    def product(at):
        xh = xhi[at]
        dims = ((1,), (0,))
        y = mul(xh, wbuf[0], dims) + (mul(xh, wbuf[1], dims) + mul(xlo[at], wbuf[0], dims))
        yh, yl = split(y)
        for s in (0, 1):
            cols = slice(s * BW, (s + 1) * BW)
            own[s, at] = y[:, cols]
            bhi[s, at, :BW] = yh[:, cols]
            blo[s, at, :BW] = yl[:, cols]

    def rows_at(begin, count):
        return pl.ds(pl.multiple_of(begin * CHUNK, CHUNK), count * CHUNK)

    def first_part(n, carry):
        k = half * part + n
        product(rows_at(k, 1))
        send(k, 0).start()
        send(k, 1).start()
        return carry

    lax.fori_loop(EARLY, EARLY + LEAD, first_part, 0)
    for s in (0, 1):
        turns[s].wait_recv()
        passed[s].start()
    lax.fori_loop(EARLY + LEAD, part, first_part, 0)

    hw = small(h, w)
    for s in (0, 1):
        gown[s] = small(w[:, s * BW:(s + 1) * BW].T, hw[:, s * BW:(s + 1) * BW])

    gpart = pl.ds(pl.multiple_of(c * (BW // 2), BW // 2), BW // 2)
    grams = [
        remote(gown.at[s, gpart], gfar.at[s, gpart], gs.at[s], gr.at[s], (partner[s], r))
        for s in (0, 1)
    ]
    grams_passed = [
        remote(gfar.at[s, gpart], gfar.at[s, gpart], gs2.at[s], gr2.at[s], sibling) for s in (0, 1)
    ]
    for cp in grams:
        cp.start()

    def second_product(n, carry):
        product(rows_at((1 - half) * part + n * (part // 2), part // 2))
        return carry

    lax.fori_loop(0, 2, second_product, 0)

    def second_start(step):
        begin = sum(PACE[:step])
        for n in range(begin, begin + PACE[step]):
            k = (1 - half) * part + n
            send(k, 0).start()
            send(k, 1).start()

    second_start(0)
    product(rows_at(half * part, EARLY))

    def cross(k, acc):
        at = pl.ds(pl.multiple_of(k * CHUNK, CHUNK), CHUNK)
        out_acc = []
        for s in (0, 1):
            lh, ll = bhi[s, at, :BW], blo[s, at, :BW]
            fh, fl = split(far[s, at])
            bhi[s, at, BW:] = fh
            blo[s, at, BW:] = fl
            dims = ((0,), (0,))
            q = mul(lh, jnp.concatenate([fh, fl], 1), dims)
            out_acc.append(acc[s] + (q[:, :BW] + (q[:, BW:] + mul(ll, fh, dims))))
        return tuple(out_acc)

    for cp in passed:
        cp.wait_recv()
    wparts = []
    for s in (0, 1):
        fh, fl = split(wfar[s])
        wparts.append((fh, jnp.concatenate([fh, fl], 1)))

    def early_chunk(n, acc):
        k = (1 - half) * part + n
        at = pl.ds(pl.multiple_of(k * CHUNK, CHUNK), CHUNK)
        came = pl.ds(pl.multiple_of(n * CHUNK, CHUNK), CHUNK)
        dims = ((1,), (0,))
        for s in (0, 1):
            early(n, s).wait_recv()
            eh, el = split(jnp.concatenate([ebuf[s, 0, came], ebuf[s, 1, came]], 1))
            q = mul(eh, wparts[s][1], dims)
            far[s, at] = q[:, :BW] + (q[:, BW:] + mul(el, wparts[s][0], dims))
        return cross(k, acc)

    def cross_chunk(n, acc):
        k = (1 - half) * part + n
        send(k, 0).wait_recv()
        send(k, 1).wait_recv()
        return cross(k, acc)

    zero = jnp.zeros((BW, BW), F32)
    acc = lax.fori_loop(0, EARLY, early_chunk, (zero, zero))
    acc = lax.fori_loop(EARLY, part, cross_chunk, acc)

    def first_wait(n, carry):
        send(half * part + n, 0).wait_send()
        send(half * part + n, 1).wait_send()
        return carry

    def early_wait(n, carry):
        early(n, 0).wait_send()
        early(n, 1).wait_send()
        return carry

    lax.fori_loop(EARLY, part, first_wait, 0)
    lax.fori_loop(0, EARLY, early_wait, 0)
    for cp in turns + passed:
        cp.wait_send()
    for s in (0, 1):
        pay2[s] = jnp.where(mine[s], acc[s], acc[s].T)
    copies = [
        remote(pay2.at[c], cbuf2.at[0], cs2.at[0], cr2.at[0], (near, r)),
        remote(pay2.at[1 - c], cbuf2.at[1], cs2.at[1], cr2.at[1], (other, aside)),
        remote(pay2.at[1 - c], cbuf2.at[2], cs2.at[2], cr2.at[2], sibling),
    ]
    for cp in copies:
        cp.start()

    second_start(1)
    for cp in copies:
        cp.wait()
    acc2[...] = (pay2[c] + cbuf2[2]) + (cbuf2[0] + cbuf2[1])
    copies = []
    for n, op in enumerate(CHIPS):
        at = pl.ds(pl.multiple_of(chip_index(op) * 8, 8), 8)
        cp = remote(acc2.at[at], rbuf2.at[n], rs2_s.at[n], rs2_r.at[n], peers[n])
        cp.start()
        copies.append(cp)
    for s in (0, 1):
        grams[s].wait_recv()
        grams_passed[s].start()
    second_start(2)
    for cp in copies:
        cp.wait()
    res2[here] = acc2[here] + jnp.sum(rbuf2[...], axis=0)
    copies = []
    for n, op in enumerate(CHIPS):
        cp = remote(res2.at[here], res2.at[here], ag2_s.at[n], ag2_r.at[n], peers[n])
        cp.start()
        copies.append(cp)
    second_start(3)
    for cp in copies:
        cp.wait()
    cp = remote(res2, full2.at[c], fs2, fr2, sibling)
    cp.start()
    second_start(4)
    full2[c] = res2[...]
    for q in grams:
        q.wait_send()
    for q in grams_passed:
        q.wait()
    cp.wait()

    items = []
    for s in (0, 1):
        first = jnp.where(mine[s], gown[s], gfar[s])
        second = jnp.where(mine[s], gfar[s], gown[s])
        fd = jnp.sum(jnp.where(i == j, first, 0.0), axis=1, keepdims=True)
        sd = jnp.sum(jnp.where(i == j, second, 0.0), axis=0, keepdims=True)
        items.append((first, second, full2[s], fd, sd))
    weights = []
    for s, (_, v) in enumerate(rotations(items)):
        v = jnp.where(lead[s], v[:, :BW], v[:, BW:])
        v = jnp.where(mine[s], v, jnp.concatenate([v[BW:], v[:BW]], 0))
        vh, vl = split(v)
        weights.append((vh, jnp.concatenate([vh, vl], 1)))

    def last_product(begin, count):
        at = rows_at(begin, count)
        dims = ((1,), (0,))
        for s in (0, 1):
            vh, vhl = weights[s]
            q = mul(bhi[s, at], vhl, dims)
            o_ref[jnp.where(uc == s, 0, 1), at] = q[:, :BW] + (q[:, BW:] + mul(blo[s, at], vh, dims))

    def last_a(n, carry):
        last_product((1 - half) * part + n * (part // 2), part // 2)
        return carry

    lax.fori_loop(0, 2, last_a, 0)

    def last_b(n, carry):
        begin = half * part + n * LAST
        at = rows_at(begin, LAST)
        for k in range(LAST):
            send(begin + k, 0).wait_recv()
            send(begin + k, 1).wait_recv()
        for s in (0, 1):
            fh, fl = split(far[s, at])
            bhi[s, at, BW:] = fh
            blo[s, at, BW:] = fl
        last_product(begin, LAST)
        return carry

    lax.fori_loop(0, part // LAST, last_b, 0)

    def finish_send(n, carry):
        k = (1 - half) * part + n
        send(k, 0).wait_send()
        send(k, 1).wait_send()
        return carry

    lax.fori_loop(0, part, finish_send, 0)


def body(matrix):
    rows = matrix.shape[1]
    n_chunks = rows // CHUNK
    dma = pltpu.SemaphoreType.DMA
    n = len(CHIPS)
    block = pltpu.VMEM((2, rows, BW), F32)
    square = pltpu.VMEM((BW, BW), F32)
    squares = pltpu.VMEM((2, BW, BW), F32)
    tile = pltpu.VMEM((8, BW), F32)
    scratch = [
        block, pltpu.VMEM((rows, 2 * BW), BF16), pltpu.VMEM((rows, 2 * BW), BF16), block, block,
        pltpu.VMEM((2, rows, 2 * BW), BF16), pltpu.VMEM((2, rows, 2 * BW), BF16),
        squares, square, tile, tile, pltpu.VMEM((16, 16, BW), F32), pltpu.VMEM((n, 16, BW), F32),
        square, squares, pltpu.VMEM((2, 2 * BW, 2 * BW), BF16),
        pltpu.VMEM((2, 2, EARLY * CHUNK, BW), F32), pltpu.VMEM((2, 2 * BW, BW), F32), pltpu.VMEM((2, 2 * BW, BW), F32),
        squares, squares, squares, pltpu.VMEM((3, BW, BW), F32), square, pltpu.VMEM((n, 8, BW), F32), square, squares,
        dma((n_chunks,)), dma((2,)), dma((2,)), dma((n,)), dma((n,)), dma((n,)), dma((n,)),
        dma, dma, dma((2, EARLY)), dma((2, EARLY)), dma((2,)), dma((2,)), dma((2,)), dma((2,)),
        dma((2, n_chunks)), dma((2, n_chunks)), dma((2,)), dma((2,)), dma((2,)), dma((2,)),
        dma((3,)), dma((3,)),
        dma((n,)), dma((n,)), dma((n,)), dma((n,)), dma, dma,
    ]
    return pl.pallas_call(
        kernel,
        out_shape=jax.ShapeDtypeStruct(matrix.shape, F32),
        in_specs=[pl.BlockSpec(memory_space=pl.ANY)],
        out_specs=pl.BlockSpec(memory_space=pltpu.VMEM),
        scratch_shapes=scratch,
        compiler_params=pltpu.CompilerParams(
            collective_id=0, has_side_effects=True, vmem_limit_bytes=48 << 20
        ),
    )(matrix)


def solution(mesh):
    specs = P(None, "row", "pair")
    return jax.shard_map(body, mesh=mesh, in_specs=(specs,), out_specs=specs, check_vma=False)
```

```python
import functools
import jax
import jax.numpy as jnp
from jax import lax
from jax.experimental import pallas as pl
from jax.experimental.pallas import tpu as pltpu
from jax.sharding import PartitionSpec as P

SWEEPS = 2
BW = 128
CHUNK = 256
EARLY = 3
PACE = (1, 1, 2, 3, 1)
LEAD = 1
LAST = 2
MESH = pl.DeviceIdType.MESH
F32 = jnp.float32
BF16 = jnp.bfloat16

CHIPS = [(a, d) for d in (4, 3, 5, 2, 6, 1, 7, 0) for a in (1, 0) if (a, d) != (0, 0)]


def split(x):
    high = x.astype(BF16)
    return high, (x - high.astype(F32)).astype(BF16)


def mul(a, b, dims):
    return lax.dot_general(a, b, (dims, ((), ())), preferred_element_type=F32)


def mul3(a, b, dims=((1,), (0,))):
    ah, al = split(a)
    bh, bl = split(b)
    return mul(ah, bh, dims) + (mul(ah, bl, dims) + mul(al, bh, dims))


def mul6(a, b, dims=((1,), (0,))):
    return lax.dot_general(
        a, b, (dims, ((), ())), precision=lax.Precision.HIGHEST, preferred_element_type=F32
    )


small = mul3


def diag_mask():
    i = lax.broadcasted_iota(jnp.int32, (BW, BW), 0)
    j = lax.broadcasted_iota(jnp.int32, (BW, BW), 1)
    return i, j


def polar_even(ts, eye):
    t2 = [small(t, t) for t in ts]
    t3 = [small(u, t) for u, t in zip(t2, ts)]
    t4 = [small(u, u) for u in t2]
    e = [0.25 * w - 0.75 * u for w, u in zip(t3, t2)]
    m = [
        eye - 0.5 * t + 0.375 * u - 0.3125 * w + 0.0625 * q
        for t, u, w, q in zip(ts, t2, t3, t4)
    ]
    s = [small(u, u) for u in e]
    r = [small(w, 0.375 * eye - 0.125 * u) for w, u in zip(m, e)]
    return [w + small(u, q) for w, u, q in zip(m, r, s)]


def turn(items, eye):
    cs = [
        cross * (1.0 / jnp.sqrt(fd + 1e-06)) * (1.0 / jnp.sqrt(sd + 1e-06))
        for cross, fd, sd in items
    ]
    totals = [jnp.sum(jnp.sum(c * c, axis=1, keepdims=True), axis=0, keepdims=True) for c in cs]
    xs = [c / (1.0 + jnp.sqrt(total)) for c, total in zip(cs, totals)]
    xts = [x.T for x in xs]
    ts = [small(x, xt) for x, xt in zip(xs, xts)] + [small(xt, x) for x, xt in zip(xs, xts)]
    evens = polar_even(ts, eye)
    n = len(items)
    return [(evens[k], small(evens[k], xs[k]), evens[n + k]) for k in range(n)]


def whole(a, b, d):
    return jnp.concatenate([jnp.concatenate([a, b], 1), jnp.concatenate([-b.T, d], 1)], 0)


def rotations(items):
    i, j = diag_mask()
    eye = jnp.where(i == j, 1.0, 0.0).astype(F32)
    hs = [
        jnp.concatenate([jnp.concatenate([f, c], 1), jnp.concatenate([c.T, s], 1)], 0)
        for f, s, c, _, _ in items
    ]
    turns = turn([item[2:] for item in items], eye)
    ys = [whole(*t) for t in turns]
    hys = [small(h, y) for h, y in zip(hs, ys)]
    crosses = [
        small(jnp.concatenate([a, -b], 1), hy[:, BW:]) for (a, b, _), hy in zip(turns, hys)
    ]
    diags = [jnp.sum(y * hy, axis=0, keepdims=True) for y, hy in zip(ys, hys)]
    firsts = [
        jnp.sum(jnp.where(i == j, diag[:, :BW], 0.0), axis=1, keepdims=True) for diag in diags
    ]
    turns = turn(
        [(c, f, diag[:, BW:]) for c, f, diag in zip(crosses, firsts, diags)], eye
    )
    return [(h, small(y, whole(*t))) for h, y, t in zip(hs, ys, turns)]


def kernel(
    x_hbm, o_ref,
    xin, xhi, xlo, own, far, bhi, blo,
    pay, cbuf, dl, dlr, rsrc, rbuf, res, full, wbuf,
    ebuf, wown, wfar, gown, gfar, pay2, cbuf2, acc2, rbuf2, res2, full2,
    lsem, cs, cr, rs_s, rs_r, ag_s, ag_r, fs, fr,
    es, er, ws, wr, ws2, wr2, ss, sr, gs, gr, gs2, gr2, cs2, cr2, rs2_s, rs2_r, ag2_s, ag2_r, fs2, fr2,
):
    p = lax.axis_index("pair")
    r = lax.axis_index("row")
    yh, z, c = r // 16, lax.rem(r // 2, 8), lax.rem(r, 2)
    chip = yh * 8 + z
    m = p // 2
    uc = lax.rem(m + 1, 2)
    half = lax.rem(m + p, 2)
    pu = jnp.where(p >= 2, p - 2, 1 - p)
    po = jnp.where(p <= 5, p + 2, 13 - p)
    partner = [jnp.where(uc == s, pu, po) for s in (0, 1)]
    mine = [jnp.where(uc == s, p == 0, p <= 6) for s in (0, 1)]
    lead = [jnp.where(uc == s, p != 1, p == 7) for s in (0, 1)]
    swap = jnp.logical_or(lax.rem(m, 2) == 1, p == 0)
    rows = x_hbm.shape[1]
    n_chunks = rows // CHUNK
    part = n_chunks // 2

    def chip_row(op, core):
        return lax.rem(yh + op[0], 2) * 16 + lax.rem(z + op[1], 8) * 2 + core

    def chip_index(op):
        return lax.rem(yh + op[0], 2) * 8 + lax.rem(z + op[1], 8)

    sibling = (p, chip_row((0, 0), 1 - c))
    peers = [(p, chip_row(op, c)) for op in CHIPS]

    def remote(src, dst, send, recv, device):
        return pltpu.make_async_remote_copy(
            src_ref=src, dst_ref=dst, send_sem=send, recv_sem=recv,
            device_id=device, device_id_type=MESH,
        )

    def load(k):
        return pltpu.make_async_copy(
            x_hbm.at[:, pl.ds(k * CHUNK, CHUNK)], xin.at[:, pl.ds(k * CHUNK, CHUNK)], lsem.at[k]
        )

    def early(n, s):
        src = pl.ds(pl.multiple_of((half * part + n) * CHUNK, CHUNK), CHUNK)
        dst = pl.ds(n * CHUNK, CHUNK)
        return remote(xin.at[:, src], ebuf.at[s, :, dst], es.at[s, n], er.at[s, n], (partner[s], r))

    for k in range(n_chunks):
        load(k).start()
    barrier = pltpu.get_barrier_semaphore()
    aside = sibling[1]
    near = jnp.where(c == 0, partner[0], partner[1])
    other = jnp.where(c == 0, partner[1], partner[0])
    everyone = [sibling] + peers + [(partner[0], r), (partner[1], r), (near, aside)]
    for device in everyone:
        pl.semaphore_signal(barrier, inc=1, device_id=device, device_id_type=MESH)

    def gram_chunk(k, g):
        load(k).wait()
        at = pl.ds(pl.multiple_of(k * CHUNK, CHUNK), CHUNK)
        high, low = split(jnp.concatenate([xin[0, at], xin[1, at]], 1))
        xhi[at] = high
        xlo[at] = low
        return g + mul(high, jnp.concatenate([high, low], 1), ((0,), (0,)))

    g = lax.fori_loop(0, n_chunks, gram_chunk, jnp.zeros((2 * BW, 4 * BW), F32))
    gl = g[:, 2 * BW:]
    g = g[:, :2 * BW] + (gl + gl.T)
    i, j = diag_mask()
    pay[0] = g[:BW, BW:]
    pay[1] = jnp.where(i >= j, g[:BW, :BW], g[BW:, BW:])
    low_diag = jnp.sum(jnp.where(i == j, g[BW:, BW:], 0.0), axis=0, keepdims=True)
    dl[...] = jnp.broadcast_to(low_diag, (8, BW))
    pl.semaphore_wait(barrier, len(everyone))

    c1 = remote(pay.at[1 - c], cbuf, cs.at[0], cr.at[0], sibling)
    c2 = remote(dl, dlr, cs.at[1], cr.at[1], sibling)
    c1.start()
    c2.start()
    c1.wait()
    c2.wait()
    rsrc[:, :8] = (pay[c] + cbuf[...]).reshape(16, 8, BW)
    rsrc[:, 8:] = jnp.broadcast_to((dl[...] + dlr[...])[None], (16, 8, BW))
    copies = []
    for n, op in enumerate(CHIPS):
        cp = remote(rsrc.at[chip_index(op)], rbuf.at[n], rs_s.at[n], rs_r.at[n], peers[n])
        cp.start()
        copies.append(cp)
    early(0, 0).start()
    early(0, 1).start()
    for cp in copies:
        cp.wait()
    total = rsrc[chip] + jnp.sum(rbuf[...], axis=0)
    low_diag = total[8:9]
    here = pl.ds(pl.multiple_of(chip * 8, 8), 8)
    res[here] = total[:8]
    copies = []
    for n, op in enumerate(CHIPS):
        cp = remote(res.at[here], res.at[here], ag_s.at[n], ag_r.at[n], peers[n])
        cp.start()
        copies.append(cp)
    early(1, 0).start()
    early(1, 1).start()
    for cp in copies:
        cp.wait()
    cp = remote(res, full.at[c], fs, fr, sibling)
    cp.start()
    for n in range(2, EARLY):
        early(n, 0).start()
        early(n, 1).start()
    full[c] = res[...]
    cp.wait()
    cross = full[0]
    packed = full[1]
    flipped = packed.T
    upper = jnp.where(i >= j, packed, flipped)
    lower = jnp.where(i == j, jnp.broadcast_to(low_diag, (BW, BW)), jnp.where(i < j, packed, flipped))
    up_diag = jnp.sum(jnp.where(i == j, upper, 0.0), axis=1, keepdims=True)
    [(h, v)] = rotations([(upper, lower, cross, up_diag, low_diag)])
    w = jnp.where(swap, jnp.concatenate([v[:, BW:], v[:, :BW]], 1), v)
    wh, wl = split(w)
    wbuf[0] = wh
    wbuf[1] = wl

    for s in (0, 1):
        wown[s] = w[:, s * BW:(s + 1) * BW]
    wpart = pl.ds(pl.multiple_of(c * BW, BW), BW)
    turns = [
        remote(wown.at[s, wpart], wfar.at[s, wpart], ws.at[s], wr.at[s], (partner[s], r))
        for s in (0, 1)
    ]
    passed = [
        remote(wfar.at[s, wpart], wfar.at[s, wpart], ws2.at[s], wr2.at[s], sibling) for s in (0, 1)
    ]
    for cp in turns:
        cp.start()

    def send(k, s):
        at = pl.ds(pl.multiple_of(k * CHUNK, CHUNK), CHUNK)
        return remote(own.at[s, at], far.at[s, at], ss.at[s, k], sr.at[s, k], (partner[s], r))

    def product(at):
        xh = xhi[at]
        dims = ((1,), (0,))
        y = mul(xh, wbuf[0], dims) + (mul(xh, wbuf[1], dims) + mul(xlo[at], wbuf[0], dims))
        yh, yl = split(y)
        for s in (0, 1):
            cols = slice(s * BW, (s + 1) * BW)
            own[s, at] = y[:, cols]
            bhi[s, at, :BW] = yh[:, cols]
            blo[s, at, :BW] = yl[:, cols]

    def rows_at(begin, count):
        return pl.ds(pl.multiple_of(begin * CHUNK, CHUNK), count * CHUNK)

    def first_part(n, carry):
        k = half * part + n
        product(rows_at(k, 1))
        send(k, 0).start()
        send(k, 1).start()
        return carry

    lax.fori_loop(EARLY, EARLY + LEAD, first_part, 0)
    for s in (0, 1):
        turns[s].wait_recv()
        passed[s].start()
    lax.fori_loop(EARLY + LEAD, part, first_part, 0)

    hw = small(h, w)
    for s in (0, 1):
        gown[s] = small(w[:, s * BW:(s + 1) * BW].T, hw[:, s * BW:(s + 1) * BW])

    gpart = pl.ds(pl.multiple_of(c * (BW // 2), BW // 2), BW // 2)
    grams = [
        remote(gown.at[s, gpart], gfar.at[s, gpart], gs.at[s], gr.at[s], (partner[s], r))
        for s in (0, 1)
    ]
    grams_passed = [
        remote(gfar.at[s, gpart], gfar.at[s, gpart], gs2.at[s], gr2.at[s], sibling) for s in (0, 1)
    ]
    for cp in grams:
        cp.start()

    def second_product(n, carry):
        product(rows_at((1 - half) * part + n * (part // 2), part // 2))
        return carry

    lax.fori_loop(0, 2, second_product, 0)

    def second_start(step):
        begin = sum(PACE[:step])
        for n in range(begin, begin + PACE[step]):
            k = (1 - half) * part + n
            send(k, 0).start()
            send(k, 1).start()

    second_start(0)
    product(rows_at(half * part, EARLY))

    def cross(k, acc):
        at = pl.ds(pl.multiple_of(k * CHUNK, CHUNK), CHUNK)
        out_acc = []
        for s in (0, 1):
            lh, ll = bhi[s, at, :BW], blo[s, at, :BW]
            fh, fl = split(far[s, at])
            bhi[s, at, BW:] = fh
            blo[s, at, BW:] = fl
            dims = ((0,), (0,))
            q = mul(lh, jnp.concatenate([fh, fl], 1), dims)
            out_acc.append(acc[s] + (q[:, :BW] + (q[:, BW:] + mul(ll, fh, dims))))
        return tuple(out_acc)

    for cp in passed:
        cp.wait_recv()
    wparts = []
    for s in (0, 1):
        fh, fl = split(wfar[s])
        wparts.append((fh, jnp.concatenate([fh, fl], 1)))

    def early_chunk(n, acc):
        k = (1 - half) * part + n
        at = pl.ds(pl.multiple_of(k * CHUNK, CHUNK), CHUNK)
        came = pl.ds(pl.multiple_of(n * CHUNK, CHUNK), CHUNK)
        dims = ((1,), (0,))
        for s in (0, 1):
            early(n, s).wait_recv()
            eh, el = split(jnp.concatenate([ebuf[s, 0, came], ebuf[s, 1, came]], 1))
            q = mul(eh, wparts[s][1], dims)
            far[s, at] = q[:, :BW] + (q[:, BW:] + mul(el, wparts[s][0], dims))
        return cross(k, acc)

    def cross_chunk(n, acc):
        k = (1 - half) * part + n
        send(k, 0).wait_recv()
        send(k, 1).wait_recv()
        return cross(k, acc)

    zero = jnp.zeros((BW, BW), F32)
    acc = lax.fori_loop(0, EARLY, early_chunk, (zero, zero))
    acc = lax.fori_loop(EARLY, part, cross_chunk, acc)

    def first_wait(n, carry):
        send(half * part + n, 0).wait_send()
        send(half * part + n, 1).wait_send()
        return carry

    def early_wait(n, carry):
        early(n, 0).wait_send()
        early(n, 1).wait_send()
        return carry

    lax.fori_loop(EARLY, part, first_wait, 0)
    lax.fori_loop(0, EARLY, early_wait, 0)
    for cp in turns + passed:
        cp.wait_send()
    for s in (0, 1):
        pay2[s] = jnp.where(mine[s], acc[s], acc[s].T)
    copies = [
        remote(pay2.at[c], cbuf2.at[0], cs2.at[0], cr2.at[0], (near, r)),
        remote(pay2.at[1 - c], cbuf2.at[1], cs2.at[1], cr2.at[1], (other, aside)),
        remote(pay2.at[1 - c], cbuf2.at[2], cs2.at[2], cr2.at[2], sibling),
    ]
    for cp in copies:
        cp.start()

    second_start(1)
    for cp in copies:
        cp.wait()
    acc2[...] = (pay2[c] + cbuf2[2]) + (cbuf2[0] + cbuf2[1])
    copies = []
    for n, op in enumerate(CHIPS):
        at = pl.ds(pl.multiple_of(chip_index(op) * 8, 8), 8)
        cp = remote(acc2.at[at], rbuf2.at[n], rs2_s.at[n], rs2_r.at[n], peers[n])
        cp.start()
        copies.append(cp)
    for s in (0, 1):
        grams[s].wait_recv()
        grams_passed[s].start()
    second_start(2)
    for cp in copies:
        cp.wait()
    res2[here] = acc2[here] + jnp.sum(rbuf2[...], axis=0)
    copies = []
    for n, op in enumerate(CHIPS):
        cp = remote(res2.at[here], res2.at[here], ag2_s.at[n], ag2_r.at[n], peers[n])
        cp.start()
        copies.append(cp)
    second_start(3)
    for cp in copies:
        cp.wait()
    cp = remote(res2, full2.at[c], fs2, fr2, sibling)
    cp.start()
    second_start(4)
    full2[c] = res2[...]
    for q in grams:
        q.wait_send()
    for q in grams_passed:
        q.wait()
    cp.wait()

    items = []
    for s in (0, 1):
        first = jnp.where(mine[s], gown[s], gfar[s])
        second = jnp.where(mine[s], gfar[s], gown[s])
        fd = jnp.sum(jnp.where(i == j, first, 0.0), axis=1, keepdims=True)
        sd = jnp.sum(jnp.where(i == j, second, 0.0), axis=0, keepdims=True)
        items.append((first, second, full2[s], fd, sd))
    weights = []
    for s, (_, v) in enumerate(rotations(items)):
        v = jnp.where(lead[s], v[:, :BW], v[:, BW:])
        v = jnp.where(mine[s], v, jnp.concatenate([v[BW:], v[:BW]], 0))
        vh, vl = split(v)
        weights.append((vh, jnp.concatenate([vh, vl], 1)))

    def last_product(begin, count):
        at = rows_at(begin, count)
        dims = ((1,), (0,))
        for s in (0, 1):
            vh, vhl = weights[s]
            q = mul(bhi[s, at], vhl, dims)
            o_ref[jnp.where(uc == s, 0, 1), at] = q[:, :BW] + (q[:, BW:] + mul(blo[s, at], vh, dims))

    def last_a(n, carry):
        last_product((1 - half) * part + n * (part // 2), part // 2)
        return carry

    lax.fori_loop(0, 2, last_a, 0)

    def last_b(n, carry):
        begin = half * part + n * LAST
        at = rows_at(begin, LAST)
        for k in range(LAST):
            send(begin + k, 0).wait_recv()
            send(begin + k, 1).wait_recv()
        for s in (0, 1):
            fh, fl = split(far[s, at])
            bhi[s, at, BW:] = fh
            blo[s, at, BW:] = fl
        last_product(begin, LAST)
        return carry

    lax.fori_loop(0, part // LAST, last_b, 0)

    def finish_send(n, carry):
        k = (1 - half) * part + n
        send(k, 0).wait_send()
        send(k, 1).wait_send()
        return carry

    lax.fori_loop(0, part, finish_send, 0)


def body(matrix):
    rows = matrix.shape[1]
    n_chunks = rows // CHUNK
    dma = pltpu.SemaphoreType.DMA
    n = len(CHIPS)
    block = pltpu.VMEM((2, rows, BW), F32)
    square = pltpu.VMEM((BW, BW), F32)
    squares = pltpu.VMEM((2, BW, BW), F32)
    tile = pltpu.VMEM((8, BW), F32)
    scratch = [
        block, pltpu.VMEM((rows, 2 * BW), BF16), pltpu.VMEM((rows, 2 * BW), BF16), block, block,
        pltpu.VMEM((2, rows, 2 * BW), BF16), pltpu.VMEM((2, rows, 2 * BW), BF16),
        squares, square, tile, tile, pltpu.VMEM((16, 16, BW), F32), pltpu.VMEM((n, 16, BW), F32),
        square, squares, pltpu.VMEM((2, 2 * BW, 2 * BW), BF16),
        pltpu.VMEM((2, 2, EARLY * CHUNK, BW), F32), pltpu.VMEM((2, 2 * BW, BW), F32), pltpu.VMEM((2, 2 * BW, BW), F32),
        squares, squares, squares, pltpu.VMEM((3, BW, BW), F32), square, pltpu.VMEM((n, 8, BW), F32), square, squares,
        dma((n_chunks,)), dma((2,)), dma((2,)), dma((n,)), dma((n,)), dma((n,)), dma((n,)),
        dma, dma, dma((2, EARLY)), dma((2, EARLY)), dma((2,)), dma((2,)), dma((2,)), dma((2,)),
        dma((2, n_chunks)), dma((2, n_chunks)), dma((2,)), dma((2,)), dma((2,)), dma((2,)),
        dma((3,)), dma((3,)),
        dma((n,)), dma((n,)), dma((n,)), dma((n,)), dma, dma,
    ]
    return pl.pallas_call(
        kernel,
        out_shape=jax.ShapeDtypeStruct(matrix.shape, F32),
        in_specs=[pl.BlockSpec(memory_space=pl.ANY)],
        out_specs=pl.BlockSpec(memory_space=pltpu.VMEM),
        scratch_shapes=scratch,
        compiler_params=pltpu.CompilerParams(
            collective_id=0, has_side_effects=True, vmem_limit_bytes=48 << 20
        ),
    )(matrix)


def solution(mesh):
    specs = P(None, "row", "pair")
    return jax.shard_map(body, mesh=mesh, in_specs=(specs,), out_specs=specs, check_vma=False)
```
